32 devices in a mesh: row: 4 (over x, core), col: 8 (over z, y).
Axes of the slice: x: 2, y: 2, z: 4, core: 2. Of those that a mesh axis runs over, the one named last changes fastest.
Arguments:
- hamiltonian: float32 [8, 128, 1024], P(None, 'row', 'col'), may hold values from -73 to 73, as said below
Outputs:
- reduced: float32 [8, 128, 1024], P(None, 'row', 'col')
The draws below stay inside these ranges and needn't reach their ends.
Inputs may be any that keep to these rules, and one draw needn't show every extreme that they name: `hamiltonian`: the matrix A0 is symmetric.
All inputs are finite; a program needn't handle non-finite values.
Results may differ from the reference program's by a relative error of at most 0.0003.
Values sent between devices are 32-bit elements; how exact they have to be, the bound alone decides.
A program may use at most 64 MiB of HBM per device.

```python
import math
import jax
import jax.numpy as jnp
from jax import lax

B = 256
CW = 128
BLOCKS = 8
N = 1024


def draw_hamiltonian(key, part):
    first_key = jax.random.fold_in(key, 11)
    normal = jax.random.truncated_normal(first_key, -5.0, 5.0, (N, N), jnp.float32)
    matrix = (normal + normal.T) * math.sqrt(0.5)
    return matrix.reshape(BLOCKS, CW, N)


def setup_inputs(seed: int = 0) -> dict:
    splits = jax.random.split(jax.random.key(seed), 2)
    return {
        "hamiltonian": draw_hamiltonian(jax.random.fold_in(splits[1], 71), 0),
    }


HIGH = lax.Precision.HIGHEST

def matmul(left_side, right_side):
    return jnp.dot(left_side.astype(jnp.float32), right_side.astype(jnp.float32), precision=HIGH, preferred_element_type=jnp.float32)

def reflect_step(matrix, first_col):
    panel_cols = matrix[:, first_col:first_col + B]
    gram_matrix = matmul(panel_cols.T, panel_cols)
    factor = jnp.linalg.cholesky(gram_matrix)
    reflector = lax.linalg.triangular_solve(factor, panel_cols, left_side=False, lower=True, transpose_a=True)
    image = matmul(matrix.T, reflector)
    corner = matmul(reflector.T, image)
    corrected = 2.0 * image - 2.0 * matmul(reflector, corner)
    return matrix - matmul(reflector, corrected.T) - matmul(corrected, reflector.T)

def reference(hamiltonian):
    matrix = hamiltonian.reshape(N, N)
    for panel_index in range(2):
        matrix = reflect_step(matrix, panel_index * B)
    return matrix.reshape(BLOCKS, CW, N)
```

```python
import jax
import jax.numpy as jnp
from jax import lax
from jax.experimental import pallas as pl
from jax.experimental.pallas import tpu as pltpu
from jax.sharding import PartitionSpec as P

B = 256
NB = 32
LANES = 128
REPLICATED_BYTES = 1 << 25
HIGHEST = lax.Precision.HIGHEST


def dot(left, right, dims, precision=HIGHEST):
    return lax.dot_general(
        left, right, (dims, ((), ())), precision=precision, preferred_element_type=jnp.float32
    )


def nn(left, right, precision=HIGHEST):
    return dot(left, right, ((1,), (0,)), precision)


def nt(left, right, precision=HIGHEST):
    return dot(left, right, ((1,), (1,)), precision)


def tn(left, right, precision=HIGHEST):
    return dot(left, right, ((0,), (0,)), precision)


def inverse_factor_kernel(gram_ref, out_ref, work_ref):
    size = gram_ref.shape[0]
    work_ref[:, :size] = gram_ref[...]
    work_ref[:, size:] = (
        lax.broadcasted_iota(jnp.int32, (size, size), 0)
        == lax.broadcasted_iota(jnp.int32, (size, size), 1)
    ).astype(jnp.float32)
    row_ids = lax.broadcasted_iota(jnp.int32, (NB, 1), 0)
    for low in range(0, size, NB):
        high = low + NB
        first = low // LANES * LANES
        last = size + -(-high // LANES) * LANES
        rows = work_ref[low:high, first:last]
        pivots = jnp.ones((NB, 1), jnp.float32)
        for j in range(NB):
            lane = low + j - first
            column = rows[:, lane : lane + 1]
            pivot = column[j : j + 1]
            pivots = jnp.where(row_ids == j, pivot, pivots)
            if j < NB - 1:
                below = jnp.where(row_ids > j, column, 0.0)
                rows = rows - below * (rows[j : j + 1] * (1.0 / pivot))
        rows = rows * lax.rsqrt(pivots)
        out_ref[low:high, :] = jnp.zeros((NB, size), jnp.float32)
        out_ref[low:high, : last - size] = rows[:, size - first :]
        if high < size:
            trailing = rows[:, high // LANES * LANES - first : size - first].T
            trailing = trailing[high % LANES :]
            work_ref[high:, first:last] -= nn(trailing, rows, HIGHEST)


def inverse_factor(gram):
    size = gram.shape[0]
    return pl.pallas_call(
        inverse_factor_kernel,
        out_shape=jax.ShapeDtypeStruct(gram.shape, jnp.float32),
        in_specs=[pl.BlockSpec(memory_space=pltpu.VMEM)],
        out_specs=pl.BlockSpec(memory_space=pltpu.VMEM),
        scratch_shapes=[pltpu.VMEM((size, 2 * size), jnp.float32)],
        cost_estimate=pl.CostEstimate(
            flops=4 * size**3 * 64, bytes_accessed=8 * size * size, transcendentals=size
        ),
    )(gram)


def from_root(block, axis, source):
    block = jnp.where(lax.axis_index(axis) == source, block, jnp.zeros_like(block))
    return lax.psum(block, axis)


def flat_rows(blocked):
    return blocked.reshape(-1, blocked.shape[-1])


def transposed_product(left_rows, right_rows):
    return jnp.dot(left_rows.T, right_rows, precision=HIGHEST, preferred_element_type=jnp.float32)


def outer_blocks(blocked, column_rows):
    return jnp.einsum("ajp,kp->ajk", blocked, column_rows, precision=HIGHEST)


def local_shared(hamiltonian):
    blocks, strip, columns = hamiltonian.shape
    col_index = lax.axis_index("col")
    owners_each = B // columns
    matrix = hamiltonian
    first_portions = []
    for owner_step in range(2 * owners_each):
        first_portions.append(from_root(hamiltonian, "col", owner_step))
    early_panels = jnp.concatenate(first_portions, axis=2)
    next_panel = early_panels[:, :, B : 2 * B]
    for panel_index in range(2):
        if panel_index == 0:
            panel_blocks = early_panels[:, :, 0:B]
        else:
            panel_blocks = next_panel
        panel_rows = flat_rows(panel_blocks)
        gram_matrix = lax.psum(transposed_product(panel_rows, panel_rows), "row")
        factor = jnp.linalg.cholesky(gram_matrix)
        reflector = lax.linalg.triangular_solve(
            factor, panel_rows, left_side=False, lower=True, transpose_a=True
        )
        reflector_blocks = reflector.reshape(blocks, strip, B)
        partial_image = transposed_product(flat_rows(matrix), reflector)
        image_piece = lax.psum_scatter(partial_image, "row", scatter_dimension=0, tiled=True)
        own_reflector = lax.dynamic_index_in_dim(reflector_blocks, col_index, 0, keepdims=False)
        reflector_cols, shared_cols = (
            lax.all_gather(own_reflector, "row", axis=0, tiled=True),
            lax.all_gather(image_piece, "row", axis=0, tiled=True),
        )
        product_own = None
        image_rows = lax.all_gather(image_piece[None], "col", axis=0, tiled=True)
        corner = lax.psum(transposed_product(reflector, flat_rows(image_rows)), "row")
        corrected = 2.0 * image_rows - 2.0 * jnp.einsum(
            "ajp,pq->ajq", reflector_blocks, corner, precision=HIGHEST
        )
        corrected_cols = 2.0 * shared_cols - 2.0 * jnp.dot(
            reflector_cols, corner, precision=HIGHEST, preferred_element_type=jnp.float32
        )
        matrix = (
            matrix
            - outer_blocks(reflector_blocks, corrected_cols)
            - outer_blocks(corrected, reflector_cols)
        )
        product_own = corrected
        if panel_index == 0:
            basis_next = reflector_blocks[owners_each : 2 * owners_each]
            product_next = product_own[owners_each : 2 * owners_each]
            basis_gathered, product_gathered = (
                lax.all_gather(basis_next, "row", axis=1, tiled=True),
                lax.all_gather(product_next, "row", axis=1, tiled=True),
            )
            next_panel = (
                next_panel
                - outer_blocks(reflector_blocks, flat_rows(product_gathered))
                - outer_blocks(product_own, flat_rows(basis_gathered))
            )
    return matrix


def local(hamiltonian):
    blocks, strip, columns = hamiltonian.shape
    if 8 * 4 * B * blocks * strip * lax.axis_size("row") > REPLICATED_BYTES:
        return local_shared(hamiltonian)
    row_index = lax.axis_index("row")
    col_index = lax.axis_index("col")
    width = strip * lax.axis_size("row")
    order = blocks * width
    each = B // width

    def panel_rows(index):
        part = hamiltonian[index * each : (index + 1) * each]
        part = lax.all_gather(part, ("row", "col"), axis=0)
        part = part.reshape(lax.axis_size("row"), lax.axis_size("col"), each, strip, columns)
        return part.transpose(2, 0, 3, 1, 4).reshape(B, order)

    def spread(piece):
        whole = lax.all_gather(piece, "col", axis=0)
        return whole.transpose(1, 0, 2).reshape(B, order)

    def own_columns(whole):
        return lax.dynamic_slice_in_dim(whole, col_index * columns, columns, 1)

    def own_rows(whole):
        whole = whole.reshape(B, blocks, width)
        mine = lax.dynamic_slice_in_dim(whole, row_index * strip, strip, 2)
        return mine.reshape(B, blocks * strip)

    panel = panel_rows(0)
    strip_cols = lax.all_gather(hamiltonian, "row", axis=1, tiled=True).reshape(order, columns)
    later = panel_rows(1)

    image = spread(nn(panel, strip_cols, HIGHEST))
    inverse = inverse_factor(nt(panel, panel, HIGHEST))
    basis = nn(inverse, panel)
    image = nn(inverse, image)
    corner = nt(basis, image)
    product = 2.0 * image - 2.0 * tn(corner, basis)

    later = (
        later
        - tn(product[:, B : 2 * B], basis)
        - tn(basis[:, B : 2 * B], product)
    )
    image2 = spread(nn(later, strip_cols, HIGHEST))
    inverse2 = inverse_factor(nt(later, later, HIGHEST))
    with_product = nt(later, product)
    with_basis = nt(later, basis)
    inner = nt(later, image2)
    inner = inner - nt(with_basis, with_product) - nt(with_product, with_basis)
    corner2 = nt(nn(inverse2, inner), inverse2)

    def second(pick):
        own_basis, own_product = pick(basis), pick(product)
        basis2 = nn(inverse2, pick(later))
        moved = pick(image2) - nn(with_product, own_basis) - nn(with_basis, own_product)
        product2 = 2.0 * nn(inverse2, moved) - 2.0 * tn(corner2, basis2)
        return own_basis, own_product, basis2, product2

    row_b1, row_p1, row_b2, row_p2 = second(own_rows)
    col_b1, col_p1, col_b2, col_p2 = second(own_columns)
    left = jnp.concatenate([row_b1, row_p1, row_b2, row_p2], axis=0)
    right = jnp.concatenate([col_p1, col_b1, col_p2, col_b2], axis=0)
    return hamiltonian - tn(left, right).reshape(hamiltonian.shape)


def solution(mesh):
    placed = (P(None, "row", "col"),)
    return jax.shard_map(
        local, mesh=mesh, in_specs=placed, out_specs=P(None, "row", "col"), check_vma=False
    )
```

```python
import jax
import jax.numpy as jnp
from jax import lax
from jax.experimental import pallas as pl
from jax.experimental.pallas import tpu as pltpu
from jax.sharding import PartitionSpec as P

B = 256
NB = 32
LANES = 128
REPLICATED_BYTES = 1 << 25
HIGHEST = lax.Precision.HIGHEST


def dot(left, right, dims, precision=HIGHEST):
    return lax.dot_general(
        left, right, (dims, ((), ())), precision=precision, preferred_element_type=jnp.float32
    )


def nn(left, right, precision=HIGHEST):
    return dot(left, right, ((1,), (0,)), precision)


def nt(left, right, precision=HIGHEST):
    return dot(left, right, ((1,), (1,)), precision)


def tn(left, right, precision=HIGHEST):
    return dot(left, right, ((0,), (0,)), precision)


def inverse_factor_kernel(gram_ref, out_ref, work_ref):
    size = gram_ref.shape[0]
    work_ref[:, :size] = gram_ref[...]
    work_ref[:, size:] = (
        lax.broadcasted_iota(jnp.int32, (size, size), 0)
        == lax.broadcasted_iota(jnp.int32, (size, size), 1)
    ).astype(jnp.float32)
    row_ids = lax.broadcasted_iota(jnp.int32, (NB, 1), 0)
    for low in range(0, size, NB):
        high = low + NB
        first = low // LANES * LANES
        last = size + -(-high // LANES) * LANES
        rows = work_ref[low:high, first:last]
        pivots = jnp.ones((NB, 1), jnp.float32)
        for j in range(NB):
            lane = low + j - first
            column = rows[:, lane : lane + 1]
            pivot = column[j : j + 1]
            pivots = jnp.where(row_ids == j, pivot, pivots)
            if j < NB - 1:
                below = jnp.where(row_ids > j, column, 0.0)
                rows = rows - below * (rows[j : j + 1] * (1.0 / pivot))
        rows = rows * lax.rsqrt(pivots)
        out_ref[low:high, :] = jnp.zeros((NB, size), jnp.float32)
        out_ref[low:high, : last - size] = rows[:, size - first :]
        if high < size:
            trailing = rows[:, high // LANES * LANES - first : size - first].T
            trailing = trailing[high % LANES :]
            work_ref[high:, first:last] -= nn(trailing, rows, HIGHEST)


def inverse_factor(gram):
    size = gram.shape[0]
    return pl.pallas_call(
        inverse_factor_kernel,
        out_shape=jax.ShapeDtypeStruct(gram.shape, jnp.float32),
        in_specs=[pl.BlockSpec(memory_space=pltpu.VMEM)],
        out_specs=pl.BlockSpec(memory_space=pltpu.VMEM),
        scratch_shapes=[pltpu.VMEM((size, 2 * size), jnp.float32)],
        cost_estimate=pl.CostEstimate(
            flops=4 * size**3 * 64, bytes_accessed=8 * size * size, transcendentals=size
        ),
    )(gram)


def from_root(block, axis, source):
    block = jnp.where(lax.axis_index(axis) == source, block, jnp.zeros_like(block))
    return lax.psum(block, axis)


def flat_rows(blocked):
    return blocked.reshape(-1, blocked.shape[-1])


def transposed_product(left_rows, right_rows):
    return jnp.dot(left_rows.T, right_rows, precision=HIGHEST, preferred_element_type=jnp.float32)


def outer_blocks(blocked, column_rows):
    return jnp.einsum("ajp,kp->ajk", blocked, column_rows, precision=HIGHEST)


def local_shared(hamiltonian):
    blocks, strip, columns = hamiltonian.shape
    col_index = lax.axis_index("col")
    owners_each = B // columns
    matrix = hamiltonian
    first_portions = []
    for owner_step in range(2 * owners_each):
        first_portions.append(from_root(hamiltonian, "col", owner_step))
    early_panels = jnp.concatenate(first_portions, axis=2)
    next_panel = early_panels[:, :, B : 2 * B]
    for panel_index in range(2):
        if panel_index == 0:
            panel_blocks = early_panels[:, :, 0:B]
        else:
            panel_blocks = next_panel
        panel_rows = flat_rows(panel_blocks)
        gram_matrix = lax.psum(transposed_product(panel_rows, panel_rows), "row")
        factor = jnp.linalg.cholesky(gram_matrix)
        reflector = lax.linalg.triangular_solve(
            factor, panel_rows, left_side=False, lower=True, transpose_a=True
        )
        reflector_blocks = reflector.reshape(blocks, strip, B)
        partial_image = transposed_product(flat_rows(matrix), reflector)
        image_piece = lax.psum_scatter(partial_image, "row", scatter_dimension=0, tiled=True)
        own_reflector = lax.dynamic_index_in_dim(reflector_blocks, col_index, 0, keepdims=False)
        reflector_cols, shared_cols = (
            lax.all_gather(own_reflector, "row", axis=0, tiled=True),
            lax.all_gather(image_piece, "row", axis=0, tiled=True),
        )
        product_own = None
        image_rows = lax.all_gather(image_piece[None], "col", axis=0, tiled=True)
        corner = lax.psum(transposed_product(reflector, flat_rows(image_rows)), "row")
        corrected = 2.0 * image_rows - 2.0 * jnp.einsum(
            "ajp,pq->ajq", reflector_blocks, corner, precision=HIGHEST
        )
        corrected_cols = 2.0 * shared_cols - 2.0 * jnp.dot(
            reflector_cols, corner, precision=HIGHEST, preferred_element_type=jnp.float32
        )
        matrix = (
            matrix
            - outer_blocks(reflector_blocks, corrected_cols)
            - outer_blocks(corrected, reflector_cols)
        )
        product_own = corrected
        if panel_index == 0:
            basis_next = reflector_blocks[owners_each : 2 * owners_each]
            product_next = product_own[owners_each : 2 * owners_each]
            basis_gathered, product_gathered = (
                lax.all_gather(basis_next, "row", axis=1, tiled=True),
                lax.all_gather(product_next, "row", axis=1, tiled=True),
            )
            next_panel = (
                next_panel
                - outer_blocks(reflector_blocks, flat_rows(product_gathered))
                - outer_blocks(product_own, flat_rows(basis_gathered))
            )
    return matrix


def local(hamiltonian):
    blocks, strip, columns = hamiltonian.shape
    if 8 * 4 * B * blocks * strip * lax.axis_size("row") > REPLICATED_BYTES:
        return local_shared(hamiltonian)
    row_index = lax.axis_index("row")
    col_index = lax.axis_index("col")
    width = strip * lax.axis_size("row")
    order = blocks * width

    def spread(piece):
        whole = lax.all_gather(piece, "col", axis=0)
        return whole.transpose(1, 0, 2).reshape(B, order)

    def own_columns(whole):
        return lax.dynamic_slice_in_dim(whole, col_index * columns, columns, 1)

    def own_rows(whole):
        whole = whole.reshape(B, blocks, width)
        mine = lax.dynamic_slice_in_dim(whole, row_index * strip, strip, 2)
        return mine.reshape(B, blocks * strip)

    strip_cols = lax.all_gather(hamiltonian, "row", axis=1, tiled=True).reshape(order, columns)
    panel = spread(strip_cols[:B])
    later = spread(strip_cols[B : 2 * B])

    image = spread(nn(panel, strip_cols, HIGHEST))
    inverse = inverse_factor(nt(panel, panel, HIGHEST))
    basis = nn(inverse, panel)
    image = nn(inverse, image)
    corner = nt(basis, image)
    product = 2.0 * image - 2.0 * tn(corner, basis)

    later = (
        later
        - tn(product[:, B : 2 * B], basis)
        - tn(basis[:, B : 2 * B], product)
    )
    image2 = spread(nn(later, strip_cols, HIGHEST))
    inverse2 = inverse_factor(nt(later, later, HIGHEST))
    with_product = nt(later, product)
    with_basis = nt(later, basis)
    inner = nt(later, image2)
    inner = inner - nt(with_basis, with_product) - nt(with_product, with_basis)
    corner2 = nt(nn(inverse2, inner), inverse2)

    def second(pick):
        own_basis, own_product = pick(basis), pick(product)
        basis2 = nn(inverse2, pick(later))
        moved = pick(image2) - nn(with_product, own_basis) - nn(with_basis, own_product)
        product2 = 2.0 * nn(inverse2, moved) - 2.0 * tn(corner2, basis2)
        return own_basis, own_product, basis2, product2

    row_b1, row_p1, row_b2, row_p2 = second(own_rows)
    col_b1, col_p1, col_b2, col_p2 = second(own_columns)
    left = jnp.concatenate([row_b1, row_p1, row_b2, row_p2], axis=0)
    right = jnp.concatenate([col_p1, col_b1, col_p2, col_b2], axis=0)
    return hamiltonian - tn(left, right).reshape(hamiltonian.shape)


def solution(mesh):
    placed = (P(None, "row", "col"),)
    return jax.shard_map(
        local, mesh=mesh, in_specs=placed, out_specs=P(None, "row", "col"), check_vma=False
    )
```
